32 devices in a mesh: grp: 2 (over y), seq: 4 (over z), outer: 4 (over x, core).
Axes of the slice: x: 2, y: 2, z: 4, core: 2. Of those that a mesh axis runs over, the one named last changes fastest.
Arguments:
- inputs: bfloat16 [32768, 512], P(('grp', 'outer', 'seq')), parts along dimension 0, may hold values from -6 to 6
- grad_out: bfloat16 [32768, 512], P(('grp', 'outer', 'seq')), parts along dimension 0, may hold values from -6 to 6
- w_query: bfloat16 [512, 512], replicated, may hold values from -0.25 to 0.25
- w_key: bfloat16 [512, 512], replicated, may hold values from -0.25 to 0.25
- w_value: bfloat16 [512, 512], replicated, may hold values from -0.25 to 0.25
- conv_taps: bfloat16 [4, 512], replicated, may hold values from -3 to 3
Outputs:
- grad_inputs: bfloat16 [32768, 512], P(('grp', 'outer', 'seq')), parts along dimension 0
- grad_wq: float32 [1024, 512], P('grp'), parts along dimension 0
- grad_wk: float32 [1024, 512], P('grp'), parts along dimension 0
- grad_wv: float32 [1024, 512], P('grp'), parts along dimension 0
- grad_conv: float32 [8, 512], P('grp'), parts along dimension 0
The draws below stay inside these ranges and needn't reach their ends.
There are 2 independent parts, one for each index of `grp`. The reference program is written for one: setup_inputs(seed, part) draws one part's arguments, and reference() takes and returns one part's arrays. A program takes and returns all parts, laid end to end along the dimension named above; an argument that names none is the same for every part. Nothing has to cross between parts.
All inputs are finite; a program needn't handle non-finite values.
Results may differ from the reference program's by a relative error of at most 0.0095.
Values may be sent and summed in bfloat16 or wider, within the bound.
A program may use at most 128 MiB of HBM per device.

```python
import math
import jax
import jax.numpy as jnp
from jax import lax

D = 512
HEADS = 8
HEAD_DIM = 64
TAPS = 4
BLOCK = 512
TOKENS = 16384


def levels(stream_key, dims, shards, least, top_value):
    def one(dim, blocks):
        steps = jax.random.uniform(jax.random.fold_in(jax.random.fold_in(stream_key, 6), dim), (blocks,), jnp.float32, least / len(shards), top_value / len(shards))
        return jnp.repeat(jnp.exp(steps), dims[dim] // blocks).reshape((-1,) + (1,) * (len(dims) - dim - 1))

    factor_of = one(*shards[0])
    for cut in shards[1:]:
        factor_of = factor_of * one(*cut)
    return factor_of


def normal_values(own_key, dims, scale, most, cuts=(), kind=jnp.bfloat16):
    factor_of = levels(own_key, dims, cuts, -0.22, 0.18) if cuts else 1.0
    result = jax.random.normal(own_key, dims, jnp.float32) * scale * factor_of
    return jnp.minimum(jnp.maximum(result, -most), most).astype(kind)


def setup_inputs(seed: int = 0, part: int = 0) -> dict:
    key_list = jax.random.split(jax.random.key(seed), 7)
    part_keys = jax.random.split(jax.random.fold_in(key_list[6], part), 7)
    return {
        "inputs": normal_values(part_keys[0], (TOKENS, D), 1.0, 6.0, ((0, 16),)),
        "grad_out": normal_values(part_keys[1], (TOKENS, D), 1.0, 6.0, ((0, 16),)),
        "w_query": normal_values(key_list[2], (D, D), D ** -0.5, 0.25),
        "w_key": normal_values(key_list[3], (D, D), D ** -0.5, 0.25),
        "w_value": normal_values(key_list[4], (D, D), D ** -0.5, 0.25),
        "conv_taps": normal_values(key_list[5], (TAPS, D), 0.5, 3.0),
    }


def split_heads(array, block_count):
    return array.reshape(block_count, BLOCK, HEADS, HEAD_DIM).astype(jnp.float32)

def rounded(array):
    return lax.optimization_barrier(array.astype(jnp.bfloat16)).astype(jnp.float32)

def block_grads(parts):
    queries, key_rows, value_rows, grad_rows, scales, state_prev, state_next = parts
    causal = jnp.arange(BLOCK)[:, None] >= jnp.arange(BLOCK)[None, :]
    highest = lax.Precision.HIGHEST
    scores = jnp.einsum('thj,shj->hts', grad_rows, value_rows)
    probe = rounded(jnp.where(causal[None], scores * scales[None, :, None], 0.0))
    grad_query = jnp.einsum('hts,shi->thi', probe, key_rows)
    grad_query = grad_query + scales[:, None, None] * jnp.einsum('thj,hij->thi', grad_rows, state_prev, precision=highest)
    grad_key = jnp.einsum('hts,thi->shi', probe, queries)
    grad_key = grad_key + jnp.einsum('shj,hij->shi', value_rows, state_next, precision=highest)
    affinity = jnp.einsum('thi,shi->hts', queries, key_rows)
    mixing = rounded(jnp.where(causal[None], affinity * scales[None, :, None], 0.0))
    grad_value = jnp.einsum('hts,thj->shj', mixing, grad_rows)
    grad_value = grad_value + jnp.einsum('shi,hij->shj', key_rows, state_next, precision=highest)
    return (grad_query.reshape(BLOCK, D).astype(jnp.bfloat16), grad_key.reshape(BLOCK, D).astype(jnp.bfloat16), grad_value.reshape(BLOCK, D).astype(jnp.bfloat16))

def reference(inputs, grad_out, w_query, w_key, w_value, conv_taps):
    seq_total = inputs.shape[0]
    block_count = seq_total // BLOCK
    highest = lax.Precision.HIGHEST
    queries = jnp.dot(inputs, w_query, preferred_element_type=jnp.float32).astype(jnp.bfloat16)
    keys_pre = jnp.dot(inputs, w_key, preferred_element_type=jnp.float32).astype(jnp.bfloat16)
    values = jnp.dot(inputs, w_value, preferred_element_type=jnp.float32).astype(jnp.bfloat16)
    taps = conv_taps.astype(jnp.float32)
    padded = jnp.concatenate([jnp.zeros((TAPS - 1, D), jnp.float32), keys_pre.astype(jnp.float32)], 0)
    keys = jnp.zeros((seq_total, D), jnp.float32)
    for tap_index in range(TAPS):
        keys = keys + taps[tap_index] * padded[TAPS - 1 - tap_index:TAPS - 1 - tap_index + seq_total]
    keys = keys.astype(jnp.bfloat16)
    position = jnp.arange(seq_total).astype(jnp.float32)
    scales = 1.0 / (jnp.sqrt(position + 1.0) * math.sqrt(HEAD_DIM))
    query_heads = split_heads(queries, block_count)
    key_heads = split_heads(keys, block_count)
    value_heads = split_heads(values, block_count)
    grad_heads = split_heads(grad_out, block_count)
    block_scales = scales.reshape(block_count, BLOCK)
    kv_blocks = jnp.einsum('nbhi,nbhj->nhij', key_heads, value_heads, precision=highest)
    qdo_blocks = jnp.einsum('nbhi,nbhj->nhij', query_heads * block_scales[:, :, None, None], grad_heads, precision=highest)
    state_prev = jnp.cumsum(kv_blocks, 0) - kv_blocks
    state_next = lax.optimization_barrier(jnp.sum(qdo_blocks, 0))[None] - jnp.cumsum(qdo_blocks, 0)
    grad_query, grad_key, grad_value = lax.map(block_grads, (query_heads, key_heads, value_heads, grad_heads, block_scales, state_prev, state_next))
    grad_query = grad_query.reshape(seq_total, D)
    grad_key = grad_key.reshape(seq_total, D)
    grad_value = grad_value.reshape(seq_total, D)
    key_grad32 = grad_key.astype(jnp.float32)
    after = jnp.concatenate([key_grad32, jnp.zeros((TAPS - 1, D), jnp.float32)], 0)
    grad_pre = jnp.zeros((seq_total, D), jnp.float32)
    tap_grads = []
    for tap_index in range(TAPS):
        grad_pre = grad_pre + taps[tap_index] * after[tap_index:tap_index + seq_total]
        tap_grads.append(lax.optimization_barrier(jnp.sum(key_grad32 * padded[TAPS - 1 - tap_index:TAPS - 1 - tap_index + seq_total], 0)))
    grad_pre = grad_pre.astype(jnp.bfloat16)
    grad_conv = jnp.stack(tap_grads, 0)
    grad_inputs = jnp.dot(grad_query, w_query.T, preferred_element_type=jnp.float32)
    grad_inputs = grad_inputs + jnp.dot(grad_pre, w_key.T, preferred_element_type=jnp.float32)
    grad_inputs = grad_inputs + jnp.dot(grad_value, w_value.T, preferred_element_type=jnp.float32)
    grad_wq = jnp.dot(inputs.T, grad_query, preferred_element_type=jnp.float32)
    grad_wk = jnp.dot(inputs.T, grad_pre, preferred_element_type=jnp.float32)
    grad_wv = jnp.dot(inputs.T, grad_value, preferred_element_type=jnp.float32)
    return (grad_inputs.astype(jnp.bfloat16), grad_wq, grad_wk, grad_wv, grad_conv)
```

```python
import functools
import math

import jax
import jax.numpy as jnp
from jax import lax
from jax.experimental import pallas as pl
from jax.experimental.pallas import tpu as pltpu
from jax.sharding import PartitionSpec as P

D = 512
HEADS = 8
HEAD_DIM = 64
TAPS = 4
BLOCK = 512
STRIP = 128
TILE = 256
PAIR = 2 * HEAD_DIM
PAIRS = D // PAIR
EDGE = 16
MESH = pl.DeviceIdType.MESH
BF = jnp.bfloat16
F32 = jnp.float32

NN = (((1,), (0,)), ((), ()))
NT = (((1,), (1,)), ((), ()))
TN = (((0,), (0,)), ((), ()))


def mm(a, b, dims):
    return lax.dot_general(a, b, dims, preferred_element_type=F32)


def kernel(
    seq_count, outer_count,
    inp, go, wq, wk, wv, taps_ref,
    gin, out, conv_out,
    kp32, q, qs, k, v, gs, gva, gqa, gka, gq, gk32, gv, gp,
    edge_k, edge_kr, edge_g, edge_gr,
    kvb, qdb, sb, rb, part, tot, trecv, so, st, sp, sn,
    wb, rc, sx, rx, sz, rz, csend, crc, crx, crz,
    edge_sem, s1_send, s1_recv, t_send, t_recv, s2_send, s2_recv, cv_c, cv_x, cv_z,
    c_sem, x_send, x_recv, z_send, z_recv, az_send, az_recv, ax_send, ax_recv, ac_sem,
):
    Z = seq_count
    X = outer_count // 2
    N = seq_count * outer_count
    length = inp.shape[0]
    blocks = length // BLOCK
    tiles = length // TILE
    r = D // N
    rows_z = PAIRS * HEAD_DIM // Z
    z = lax.axis_index("seq")
    o = lax.axis_index("outer")
    x, core = o // 2, o % 2
    me = o * Z + z

    def at(place):
        return {"seq": place % Z, "outer": place // Z}

    def others(count, mine, body):
        def one(i, carry):
            @pl.when(i != mine)
            def _():
                body(i)
            return carry
        lax.fori_loop(0, count, one, 0)

    def remote(src, dst, send, recv, device):
        return pltpu.make_async_remote_copy(
            src_ref=src, dst_ref=dst, send_sem=send, recv_sem=recv,
            device_id=device, device_id_type=MESH,
        )

    barrier = pltpu.get_barrier_semaphore()
    after, ahead = (me + 1) % N, (me + N - 1) % N

    def greet(device):
        pl.semaphore_signal(barrier, inc=1, device_id=device, device_id_type=MESH)

    others(Z, z, lambda i: greet({"seq": i}))
    others(outer_count, o, lambda i: greet({"outer": i}))
    greet(at(after))
    greet(at(ahead))

    lane = lax.broadcasted_iota(jnp.int32, (1, PAIR), 1)
    low = jnp.where(lane < HEAD_DIM, 1.0, 0.0)
    high = 1.0 - low
    masks = (low.astype(BF), high.astype(BF))

    kp32[8 : 8 + length, :] = mm(inp[...], wk[...], NN).astype(BF).astype(F32)
    edge_k[...] = kp32[8 + length - EDGE : 8 + length, :].astype(BF)

    pl.semaphore_wait(barrier, Z + outer_count)
    send_k = remote(edge_k, edge_kr, edge_sem.at[0], edge_sem.at[1], at(after))
    send_k.start()

    q[...] = mm(inp[...], wq[...], NN).astype(BF)
    v[...] = mm(inp[...], wv[...], NN).astype(BF)
    for i in range(tiles):
        rows = slice(i * TILE, (i + 1) * TILE)
        place = lax.broadcasted_iota(jnp.int32, (TILE, 128), 0) + (me * length + i * TILE)
        scale = 1.0 / (jnp.sqrt(place.astype(F32) + 1.0) * math.sqrt(HEAD_DIM))
        scale = jnp.concatenate([scale] * (D // 128), 1)
        qs[rows, :] = (q[rows, :].astype(F32) * scale).astype(BF)
        gs[rows, :] = (go[rows, :].astype(F32) * scale).astype(BF)
    taps = taps_ref[...].astype(F32)
    send_k.wait()
    keep = jnp.where(me == 0, 0.0, 1.0)
    kp32[0:8, :] = edge_kr[EDGE - 8 : EDGE, :].astype(F32) * keep

    for i in range(tiles):
        start = i * TILE
        rows = kp32[start : start + TILE + 8, :]
        total = taps[0:1] * rows[8 : 8 + TILE]
        for j in range(1, TAPS):
            total = total + taps[j : j + 1] * rows[8 - j : 8 - j + TILE]
        k[start : start + TILE, :] = total.astype(BF)

    def shrink(full):
        return full[:HEAD_DIM] * low + full[HEAD_DIM:] * high

    for p in range(PAIRS):
        cols = slice(p * PAIR, (p + 1) * PAIR)
        kv_sum = qd_sum = None
        for b in range(blocks):
            rows = slice(b * BLOCK, (b + 1) * BLOCK)
            kv = shrink(mm(k[rows, cols], v[rows, cols], TN))
            qd = shrink(mm(qs[rows, cols], go[rows, cols], TN))
            kvb[b, p] = kv
            qdb[b, p] = qd
            kv_sum = kv if kv_sum is None else kv_sum + kv
            qd_sum = qd if qd_sum is None else qd_sum + qd
        per = HEAD_DIM // rows_z
        for u in range(per):
            cut = slice(u * rows_z, (u + 1) * rows_z)
            sb[p * per + u, 0] = kv_sum[cut].astype(BF)
            sb[p * per + u, 1] = qd_sum[cut].astype(BF)

    def to_owner(i, source):
        return remote(sb.at[i], rb.at[source], s1_send.at[i], s1_recv.at[source], {"seq": i})

    def to_outer(i, source):
        return remote(tot, trecv.at[source], t_send.at[i], t_recv.at[source], {"outer": i})

    def to_member(i, source):
        return remote(so.at[i], st.at[source], s2_send.at[i], s2_recv.at[source], {"seq": i})

    others(Z, z, lambda i: to_owner(i, z).start())

    row = lax.broadcasted_iota(jnp.int32, (STRIP, 2 * STRIP), 0)
    col = lax.broadcasted_iota(jnp.int32, (STRIP, 2 * STRIP), 1) % STRIP

    def attend(first, second, third, keys_first, b, p):
        lanes = slice(p * PAIR, (p + 1) * PAIR)
        base = b * BLOCK
        causal = row <= col if keys_first else row >= col
        whole = first[base : base + BLOCK, lanes]
        strips = BLOCK // STRIP
        total = None
        for j in reversed(range(strips)) if keys_first else range(strips):
            cut = slice(base + j * STRIP, base + (j + 1) * STRIP)
            b_part, c_part = second[cut, lanes], third[cut, lanes]
            right = jnp.concatenate([b_part * mask for mask in masks], 0)
            weights = jnp.concatenate([c_part * mask for mask in masks], 0)
            if keys_first:
                last = (j + 1) * STRIP
                score = mm(whole[:last], right, NT)
                part = jnp.where(causal, score[j * STRIP :], 0.0).astype(BF)
                if j > 0:
                    part = jnp.concatenate([score[: j * STRIP].astype(BF), part], 0)
                res = mm(part, weights, NN)
                if total is None:
                    total = res
                else:
                    total = jnp.concatenate([total[:last] + res, total[last:]], 0)
            else:
                begin = j * STRIP
                score = mm(whole[begin:], right, NT)
                part = jnp.where(causal, score[:STRIP], 0.0).astype(BF)
                if j < strips - 1:
                    part = jnp.concatenate([part, score[STRIP:].astype(BF)], 0)
                res = mm(part, weights, NN)
                if total is None:
                    total = res
                else:
                    total = jnp.concatenate([total[:begin], total[begin:] + res], 0)
        return total

    spots = [
        (b, p, slice(b * BLOCK, (b + 1) * BLOCK), slice(p * PAIR, (p + 1) * PAIR))
        for b in range(blocks) for p in range(PAIRS)
    ]

    def values_inside():
        for b, p, rows, lanes in spots:
            gva[rows, lanes] = attend(k, qs, go, True, b, p)

    def keys_inside():
        for b, p, rows, lanes in spots:
            gka[rows, lanes] = attend(v, gs, q, True, b, p)

    def queries_inside():
        for b, p, rows, lanes in spots:
            gqa[rows, lanes] = attend(gs, v, k, False, b, p)

    values_inside()


    others(Z, z, lambda i: to_owner(i, i).wait_recv())
    rb[z] = sb[z]
    total = jnp.zeros((rows_z, PAIR), F32)
    for i in range(Z):
        part[i, 0] = total
        total = total + rb[i, 0].astype(F32)
    tot[0] = total.astype(BF)
    total = jnp.zeros((rows_z, PAIR), F32)
    for i in reversed(range(Z)):
        part[i, 1] = total
        total = total + rb[i, 1].astype(F32)
    tot[1] = total.astype(BF)
    others(outer_count, o, lambda i: to_outer(i, o).start())
    keys_inside()
    others(outer_count, o, lambda i: to_outer(i, i).wait_recv())
    trecv[o] = tot[...]
    earlier = jnp.zeros((rows_z, PAIR), F32)
    later = jnp.zeros((rows_z, PAIR), F32)
    for i in range(outer_count):
        earlier = earlier + trecv[i, 0].astype(F32) * jnp.where(i < o, 1.0, 0.0)
        later = later + trecv[i, 1].astype(F32) * jnp.where(i > o, 1.0, 0.0)
    for i in range(Z):
        so[i, 0] = (earlier + part[i, 0]).astype(BF)
        so[i, 1] = (later + part[i, 1]).astype(BF)
    st[z] = so[z]
    others(Z, z, lambda i: to_member(i, z).start())

    queries_inside()
    others(Z, z, lambda i: to_member(i, i).wait_recv())

    per = HEAD_DIM // rows_z
    for p in range(PAIRS):
        prev = st[p * per : (p + 1) * per, 0].astype(F32).reshape(HEAD_DIM, PAIR)
        for b in range(blocks):
            sp[b, p] = jnp.concatenate([prev * low, prev * high], 0).astype(BF)
            prev = prev + kvb[b, p]
        later = st[p * per : (p + 1) * per, 1].astype(F32).reshape(HEAD_DIM, PAIR)
        for b in reversed(range(blocks)):
            sn[b, p] = jnp.concatenate([later * low, later * high], 0).astype(BF)
            later = later + qdb[b, p]

    for b, p, rows, lanes in spots:
        gk32[rows, lanes] = (gka[rows, lanes] + mm(v[rows, lanes], sn[b, p], NT)).astype(BF).astype(F32)
    edge_g[...] = gk32[0:EDGE, :].astype(BF)
    send_g = remote(edge_g, edge_gr, edge_sem.at[2], edge_sem.at[3], at(ahead))
    send_g.start()
    for b, p, rows, lanes in spots:
        gv[rows, lanes] = (gva[rows, lanes] + mm(k[rows, lanes], sn[b, p], NN)).astype(BF)

    def weight(c, grads):
        res = mm(inp[...], grads[...], TN).astype(BF)
        for i in range(2 * X * Z):
            wb[c, i // (X * Z), i // Z % X, i % Z] = res[r * i : r * i + r]

    def core_copy(c):
        return remote(wb.at[c, 1 - core], rc.at[c], c_sem.at[c, 0], c_sem.at[c, 1],
                      {"outer": x * 2 + 1 - core})

    def x_copy(c, i, source):
        return remote(sx.at[c, i], rx.at[c, source], x_send.at[c, i], x_recv.at[c, source],
                      {"outer": i * 2 + core})

    def z_copy(c, i, source):
        return remote(sz.at[c, i], rz.at[c, source], z_send.at[c, i], z_recv.at[c, source],
                      {"seq": i})

    def az_copy(c, i, source):
        slot = out.at[c, core, x, source]
        return remote(slot, slot, az_send.at[c, i], az_recv.at[c, source], {"seq": i})

    def ax_copy(c, i, source):
        slot = out.at[c, core, source]
        return remote(slot, slot, ax_send.at[c, i], ax_recv.at[c, source],
                      {"outer": i * 2 + core})

    def ac_copy(c, source):
        slot = out.at[c, source]
        return remote(slot, slot, ac_sem.at[c, 0], ac_sem.at[c, 1],
                      {"outer": x * 2 + 1 - core})

    def stage_core(c):
        core_copy(c).start()

    def stage_x(c):
        core_copy(c).wait_recv()
        for i in range(X):
            sx[c, i] = (wb[c, core, i].astype(F32) + rc[c, i].astype(F32)).astype(BF)
        others(X, x, lambda i: x_copy(c, i, x).start())

    def stage_z(c):
        others(X, x, lambda i: x_copy(c, i, i).wait_recv())
        rx[c, x] = sx[c, x]
        total = rx[c, 0].astype(F32)
        for i in range(1, X):
            total = total + rx[c, i].astype(F32)
        sz[c] = total.astype(BF)
        others(Z, z, lambda i: z_copy(c, i, z).start())

    def stage_az(c):
        others(Z, z, lambda i: z_copy(c, i, i).wait_recv())
        rz[c, z] = sz[c, z]
        total = rz[c, 0].astype(F32)
        for i in range(1, Z):
            total = total + rz[c, i].astype(F32)
        out[c, core, x, z] = total.astype(BF)
        others(Z, z, lambda i: az_copy(c, i, z).start())

    def stage_ax(c):
        others(Z, z, lambda i: az_copy(c, i, i).wait_recv())
        others(X, x, lambda i: ax_copy(c, i, x).start())

    def stage_ac(c):
        others(X, x, lambda i: ax_copy(c, i, i).wait_recv())
        ac_copy(c, core).start()

    def stage_end(c):
        ac_copy(c, 1 - core).wait_recv()
        core_copy(c).wait_send()
        others(X, x, lambda i: x_copy(c, i, x).wait_send())
        others(Z, z, lambda i: z_copy(c, i, z).wait_send())
        others(Z, z, lambda i: az_copy(c, i, z).wait_send())
        others(X, x, lambda i: ax_copy(c, i, x).wait_send())
        ac_copy(c, core).wait_send()

    weight(0, gv)
    stage_core(0)

    for b, p, rows, lanes in spots:
        gq[rows, lanes] = (gqa[rows, lanes] + mm(gs[rows, lanes], sp[b, p], NT)).astype(BF)
    stage_x(0)
    weight(1, gq)
    stage_core(1)
    send_g.wait()
    keep_g = jnp.where(me == N - 1, 0.0, 1.0)
    gk32[length : length + 8, :] = edge_gr[0:8, :].astype(F32) * keep_g

    sums = [jnp.zeros((8, D), F32)] * TAPS
    for i in range(tiles):
        start = i * TILE
        rows = gk32[start : start + TILE + 8, :]
        keys = kp32[start : start + TILE + 8, :]
        own = rows[0:TILE]
        total = taps[0:1] * own
        for j in range(1, TAPS):
            total = total + taps[j : j + 1] * rows[j : j + TILE]
        gp[start : start + TILE, :] = total.astype(BF)
        sums = [
            sums[j] + jnp.sum((own * keys[8 - j : 8 - j + TILE]).reshape(TILE // 8, 8, D), 0)
            for j in range(TAPS)
        ]
    for j in range(TAPS):
        csend[0, j : j + 1, :] = jnp.sum(sums[j], 0, keepdims=True)

    conv_core = remote(csend.at[0], crc, cv_c.at[0], cv_c.at[1], {"outer": x * 2 + 1 - core})

    def conv_x(i, source):
        return remote(csend.at[1], crx.at[source], cv_x.at[0, i], cv_x.at[1, source],
                      {"outer": i * 2 + core})

    def conv_z(i, source):
        return remote(csend.at[2], crz.at[source], cv_z.at[0, i], cv_z.at[1, source], {"seq": i})

    stage_x(1)
    weight(2, gp)
    stage_core(2)
    conv_core.start()
    stage_z(0)

    def gin_part(part):
        rows = slice(part * length // 2, (part + 1) * length // 2)
        total = mm(gq[rows, :], wq[...], NT)
        total = total + mm(gv[rows, :], wv[...], NT)
        total = total + mm(gp[rows, :], wk[...], NT)
        gin[rows, :] = total.astype(BF)

    gin_part(0)
    stage_x(2)
    conv_core.wait_recv()
    csend[1] = csend[0] + crc[...]
    others(X, x, lambda i: conv_x(i, x).start())
    gin_part(1)
    stage_z(1)
    stage_az(0)
    stage_z(2)
    stage_az(1)
    stage_ax(0)
    stage_az(2)
    stage_ac(0)
    stage_ax(1)
    others(X, x, lambda i: conv_x(i, i).wait_recv())
    crx[x] = csend[1]
    total = crx[0]
    for i in range(1, X):
        total = total + crx[i]
    csend[2] = total
    others(Z, z, lambda i: conv_z(i, z).start())
    stage_ax(2)
    stage_ac(1)
    stage_ac(2)
    others(Z, z, lambda i: conv_z(i, i).wait_recv())
    crz[z] = csend[2]
    total = crz[0]
    for i in range(1, Z):
        total = total + crz[i]
    conv_out[...] = total
    others(Z, z, lambda i: to_owner(i, z).wait_send())
    others(outer_count, o, lambda i: to_outer(i, o).wait_send())
    others(Z, z, lambda i: to_member(i, z).wait_send())
    conv_core.wait_send()
    others(X, x, lambda i: conv_x(i, x).wait_send())
    others(Z, z, lambda i: conv_z(i, z).wait_send())
    stage_end(0)
    stage_end(1)
    stage_end(2)


def on_device(seq_count, outer_count, inputs, grad_out, w_query, w_key, w_value, conv_taps):
    length = inputs.shape[0]
    Z, X = seq_count, outer_count // 2
    N = seq_count * outer_count
    r = D // N
    blocks = length // BLOCK
    vm = pltpu.VMEM
    dma = pltpu.SemaphoreType.DMA
    full = vm((length, D), BF)
    edge = vm((EDGE, D), BF)
    state = vm((blocks, PAIRS, HEAD_DIM, PAIR), F32)
    rows_z = PAIRS * HEAD_DIM // Z
    sliced = vm((Z, 2, rows_z, PAIR), BF)
    parts = vm((Z, 2, rows_z, PAIR), F32)
    total = vm((2, rows_z, PAIR), BF)
    totals = vm((outer_count, 2, rows_z, PAIR), BF)
    square = vm((blocks, PAIRS, PAIR, PAIR), BF)
    scratch = [
        vm((length + 8, D), F32), full, full, full, full, full,
        vm((length, D), F32), vm((length, D), F32), vm((length, D), F32), full, vm((length + 8, D), F32), full, full,
        edge, edge, edge, edge,
        state, state, sliced, sliced, parts, total, totals, sliced, sliced, square, square,
        vm((3, 2, X, Z, r, D), BF), vm((3, X, Z, r, D), BF), vm((3, X, Z, r, D), BF),
        vm((3, X, Z, r, D), BF), vm((3, Z, r, D), BF), vm((3, Z, r, D), BF),
        vm((3, TAPS, D), F32), vm((TAPS, D), F32), vm((X, TAPS, D), F32), vm((Z, TAPS, D), F32),
        dma((4,)), dma((Z,)), dma((Z,)), dma((outer_count,)), dma((outer_count,)), dma((Z,)), dma((Z,)),
        dma((2,)), dma((2, X)), dma((2, Z)),
        dma((3, 2)), dma((3, X)), dma((3, X)), dma((3, Z)), dma((3, Z)),
        dma((3, Z)), dma((3, Z)), dma((3, X)), dma((3, X)), dma((3, 2)),
    ]
    spec = pl.BlockSpec(memory_space=pltpu.VMEM)
    grad_inputs, weights, grad_conv = pl.pallas_call(
        functools.partial(kernel, seq_count, outer_count),
        out_shape=(
            jax.ShapeDtypeStruct((length, D), BF),
            jax.ShapeDtypeStruct((3, 2, X, Z, r, D), BF),
            jax.ShapeDtypeStruct((TAPS, D), F32),
        ),
        in_specs=[spec] * 6,
        out_specs=(spec, spec, spec),
        scratch_shapes=scratch,
        compiler_params=pltpu.CompilerParams(
            collective_id=0, has_side_effects=True, vmem_limit_bytes=56 * 1024 * 1024
        ),
    )(inputs, grad_out, w_query, w_key, w_value, conv_taps)
    weights = weights.reshape(3, D, D).astype(F32)
    return (grad_inputs, weights[1], weights[2], weights[0], grad_conv)


def solution(mesh):
    rows = P(("grp", "outer", "seq"), None)
    body = functools.partial(on_device, mesh.shape["seq"], mesh.shape["outer"])
    return jax.shard_map(
        body,
        mesh=mesh,
        in_specs=(rows, rows, P(), P(), P(), P()),
        out_specs=(rows, P("grp", None), P("grp", None), P("grp", None), P("grp", None)),
        check_vma=False,
    )
```

```python
import functools
import math

import jax
import jax.numpy as jnp
from jax import lax
from jax.experimental import pallas as pl
from jax.experimental.pallas import tpu as pltpu
from jax.sharding import PartitionSpec as P

D = 512
HEADS = 8
HEAD_DIM = 64
TAPS = 4
BLOCK = 512
STRIP = 128
TILE = 256
PAIR = 2 * HEAD_DIM
PAIRS = D // PAIR
EDGE = 16
MESH = pl.DeviceIdType.MESH
BF = jnp.bfloat16
F32 = jnp.float32

NN = (((1,), (0,)), ((), ()))
NT = (((1,), (1,)), ((), ()))
TN = (((0,), (0,)), ((), ()))


def mm(a, b, dims):
    return lax.dot_general(a, b, dims, preferred_element_type=F32)


def kernel(
    seq_count, outer_count,
    inp_hbm, go_hbm, wq_hbm, wk_hbm, wv_hbm, taps_hbm,
    gin_hbm, out_hbm, conv_hbm,
    inp, go, wq, wk, wv, taps_ref, gin, out, conv_out,
    kp32, q, qs, k, v, gs, gva, gqa, gka, gq, gk32, gv, gp,
    edge_k, edge_g, edge_gr,
    kvb, qdb, sb, rb, so, st, sp, sn,
    wb, rc, sx, rx, sz, rz, csend, crc, crx, crz,
    edge_sem, s1_send, s1_recv, s2_send, s2_recv, cv_c, cv_x, cv_z,
    c_sem, x_send, x_recv, z_send, z_recv, az_send, az_recv, ax_send, ax_recv, ac_sem,
    in_sem, out_sem,
):
    Z = seq_count
    X = outer_count // 2
    N = seq_count * outer_count
    length = inp.shape[0]
    blocks = length // BLOCK
    tiles = length // TILE
    r = D // N
    share = PAIRS * HEAD_DIM // N
    z = lax.axis_index("seq")
    o = lax.axis_index("outer")
    x, core = o // 2, o % 2
    me = o * Z + z

    def at(place):
        return {"seq": place % Z, "outer": place // Z}

    def others(count, mine, body):
        def one(i, carry):
            @pl.when(i != mine)
            def _():
                body(i)
            return carry
        lax.fori_loop(0, count, one, 0)

    def remote(src, dst, send, recv, device):
        return pltpu.make_async_remote_copy(
            src_ref=src, dst_ref=dst, send_sem=send, recv_sem=recv,
            device_id=device, device_id_type=MESH,
        )

    def peers(body):
        def one(i, carry):
            body(lax.rem(me + i, N))
            return carry
        lax.fori_loop(1, N, one, 0, unroll=N <= 16)

    operands = (
        (inp_hbm, inp), (wq_hbm, wq), (go_hbm, go), (wk_hbm, wk), (wv_hbm, wv), (taps_hbm, taps_ref)
    )
    loads = [pltpu.make_async_copy(a, b, in_sem.at[i]) for i, (a, b) in enumerate(operands)]
    for load in loads:
        load.start()
    inp_load, wq_load, go_load, wk_load, wv_load, taps_load = loads

    barrier = pltpu.get_barrier_semaphore()
    after, ahead = (me + 1) % N, (me + N - 1) % N

    def greet(place):
        pl.semaphore_signal(barrier, inc=1, device_id=at(place), device_id_type=MESH)

    peers(greet)

    lane = lax.broadcasted_iota(jnp.int32, (1, PAIR), 1)
    low = jnp.where(lane < HEAD_DIM, 1.0, 0.0)
    high = 1.0 - low
    masks = (low.astype(BF), high.astype(BF))

    inp_load.wait()
    wq_load.wait()
    q[...] = mm(inp[...], wq[...], NN).astype(BF)
    go_load.wait()
    for i in range(tiles):
        rows = slice(i * TILE, (i + 1) * TILE)
        place = lax.broadcasted_iota(jnp.int32, (TILE, 128), 0) + (me * length + i * TILE)
        scale = 1.0 / (jnp.sqrt(place.astype(F32) + 1.0) * math.sqrt(HEAD_DIM))
        scale = jnp.concatenate([scale] * (D // 128), 1)
        qs[rows, :] = (q[rows, :].astype(F32) * scale).astype(BF)
        gs[rows, :] = (go[rows, :].astype(F32) * scale).astype(BF)

    def shrink(full):
        return full[:HEAD_DIM] * low + full[HEAD_DIM:] * high

    def block_states(kind, first, second, kept):
        for p in range(PAIRS):
            cols = slice(p * PAIR, (p + 1) * PAIR)
            total = None
            for b in range(blocks):
                rows = slice(b * BLOCK, (b + 1) * BLOCK)
                one = shrink(mm(first[rows, cols], second[rows, cols], TN))
                kept[b, p] = one
                total = one if total is None else total + one
            per = HEAD_DIM // share
            sb[kind, p * per : (p + 1) * per] = total.reshape(per, share, PAIR).astype(BF)

    def to_owner(kind, i):
        return remote(sb.at[kind, i], rb.at[kind, me], s1_send.at[kind], s1_recv.at[kind], at(i))

    def to_member(kind, i):
        return remote(so.at[kind, i], st.at[kind, me], s2_send.at[kind], s2_recv.at[kind], at(i))

    def take(buffer, kind, sem):
        whole = buffer.at[kind, pl.ds(0, N - 1)]
        pltpu.make_async_copy(whole, whole, sem.at[kind]).wait()

    def send_states(kind):
        rb[kind, me] = sb[kind, me]
        peers(lambda i: to_owner(kind, i).start())

    def return_states(kind):
        take(rb, kind, s1_recv)
        total = jnp.zeros((share, PAIR), F32)
        for i in reversed(range(N)) if kind else range(N):
            so[kind, i] = total.astype(BF)
            total = total + rb[kind, i].astype(F32)
        st[kind, me] = so[kind, me]
        peers(lambda i: to_member(kind, i).start())

    block_states(1, qs, go, qdb)
    pl.semaphore_wait(barrier, N - 1)
    send_k = remote(inp_hbm.at[length - EDGE : length], edge_k, edge_sem.at[0], edge_sem.at[1], at(after))
    send_k.start()
    send_states(1)
    wk_load.wait()
    kp32[8 : 8 + length, :] = mm(inp[...], wk[...], NN).astype(BF).astype(F32)
    wv_load.wait()
    v[...] = mm(inp[...], wv[...], NN).astype(BF)
    taps_load.wait()
    taps = taps_ref[...].astype(F32)
    send_k.wait()
    keep = jnp.where(me == 0, 0.0, 1.0)
    edge = mm(edge_k[...], wk[...], NN).astype(BF).astype(F32)
    kp32[0:8, :] = edge[EDGE - 8 : EDGE] * keep
    for i in range(tiles):
        start = i * TILE
        rows = kp32[start : start + TILE + 8, :]
        total = taps[0:1] * rows[8 : 8 + TILE]
        for j in range(1, TAPS):
            total = total + taps[j : j + 1] * rows[8 - j : 8 - j + TILE]
        k[start : start + TILE, :] = total.astype(BF)

    block_states(0, k, v, kvb)
    send_states(0)

    row = lax.broadcasted_iota(jnp.int32, (STRIP, 2 * STRIP), 0)
    col = lax.broadcasted_iota(jnp.int32, (STRIP, 2 * STRIP), 1) % STRIP

    def attend(first, second, third, keys_first, b, p):
        lanes = slice(p * PAIR, (p + 1) * PAIR)
        base = b * BLOCK
        causal = row <= col if keys_first else row >= col
        whole = first[base : base + BLOCK, lanes]
        strips = BLOCK // STRIP
        total = None
        for j in reversed(range(strips)) if keys_first else range(strips):
            cut = slice(base + j * STRIP, base + (j + 1) * STRIP)
            b_part, c_part = second[cut, lanes], third[cut, lanes]
            right = jnp.concatenate([b_part * mask for mask in masks], 0)
            weights = jnp.concatenate([c_part * mask for mask in masks], 0)
            if keys_first:
                last = (j + 1) * STRIP
                score = mm(whole[:last], right, NT)
                part = jnp.where(causal, score[j * STRIP :], 0.0).astype(BF)
                if j > 0:
                    part = jnp.concatenate([score[: j * STRIP].astype(BF), part], 0)
                res = mm(part, weights, NN)
                if total is None:
                    total = res
                else:
                    total = jnp.concatenate([total[:last] + res, total[last:]], 0)
            else:
                begin = j * STRIP
                score = mm(whole[begin:], right, NT)
                part = jnp.where(causal, score[:STRIP], 0.0).astype(BF)
                if j < strips - 1:
                    part = jnp.concatenate([part, score[STRIP:].astype(BF)], 0)
                res = mm(part, weights, NN)
                if total is None:
                    total = res
                else:
                    total = jnp.concatenate([total[:begin], total[begin:] + res], 0)
        return total

    spots = [
        (b, p, slice(b * BLOCK, (b + 1) * BLOCK), slice(p * PAIR, (p + 1) * PAIR))
        for b in range(blocks) for p in range(PAIRS)
    ]

    def inside(total, first, second, third, keys_first, part):
        for b, p, rows, lanes in spots[part * len(spots) // 2 : (part + 1) * len(spots) // 2]:
            total[rows, lanes] = attend(first, second, third, keys_first, b, p)

    per = HEAD_DIM // share

    def from_parts(kind, p):
        return st[kind, p * per : (p + 1) * per].astype(F32).reshape(HEAD_DIM, PAIR)

    inside(gva, k, qs, go, True, 0)
    return_states(1)
    inside(gva, k, qs, go, True, 1)
    inside(gka, v, gs, q, True, 0)
    return_states(0)
    inside(gka, v, gs, q, True, 1)

    take(st, 1, s2_recv)
    for p in range(PAIRS):
        later = from_parts(1, p)
        for b in reversed(range(blocks)):
            sn[b, p] = jnp.concatenate([later * low, later * high], 0).astype(BF)
            later = later + qdb[b, p]

    for b, p, rows, lanes in spots:
        gk32[rows, lanes] = (gka[rows, lanes] + mm(v[rows, lanes], sn[b, p], NT)).astype(BF).astype(F32)
    edge_g[...] = gk32[0:EDGE, :].astype(BF)
    send_g = remote(edge_g, edge_gr, edge_sem.at[2], edge_sem.at[3], at(ahead))
    send_g.start()
    for b, p, rows, lanes in spots:
        gv[rows, lanes] = (gva[rows, lanes] + mm(k[rows, lanes], sn[b, p], NN)).astype(BF)

    def weight(c, grads):
        res = mm(inp[...], grads[...], TN).astype(BF)
        for i in range(2 * X * Z):
            wb[c, i // (X * Z), i // Z % X, i % Z] = res[r * i : r * i + r]

    def core_copy(c):
        return remote(wb.at[c, 1 - core], rc.at[c], c_sem.at[c, 0], c_sem.at[c, 1],
                      {"outer": x * 2 + 1 - core})

    def x_copy(c, i, source):
        return remote(sx.at[c, i], rx.at[c, source], x_send.at[c, i], x_recv.at[c, source],
                      {"outer": i * 2 + core})

    def z_copy(c, i, source):
        return remote(sz.at[c, i], rz.at[c, source], z_send.at[c, i], z_recv.at[c, source],
                      {"seq": i})

    def az_copy(c, i, source):
        slot = out.at[c, core, x, source]
        return remote(slot, slot, az_send.at[c, i], az_recv.at[c, source], {"seq": i})

    def ax_copy(c, i, source):
        slot = out.at[c, core, source]
        return remote(slot, slot, ax_send.at[c, i], ax_recv.at[c, source],
                      {"outer": i * 2 + core})

    def ac_copy(c, source):
        slot = out.at[c, source]
        return remote(slot, slot, ac_sem.at[c, 0], ac_sem.at[c, 1],
                      {"outer": x * 2 + 1 - core})

    def stage_core(c):
        core_copy(c).start()

    def stage_x(c):
        core_copy(c).wait_recv()
        for i in range(X):
            sx[c, i] = (wb[c, core, i].astype(F32) + rc[c, i].astype(F32)).astype(BF)
        others(X, x, lambda i: x_copy(c, i, x).start())

    def stage_z(c):
        others(X, x, lambda i: x_copy(c, i, i).wait_recv())
        rx[c, x] = sx[c, x]
        total = rx[c, 0].astype(F32)
        for i in range(1, X):
            total = total + rx[c, i].astype(F32)
        sz[c] = total.astype(BF)
        others(Z, z, lambda i: z_copy(c, i, z).start())

    def stage_az(c):
        others(Z, z, lambda i: z_copy(c, i, i).wait_recv())
        rz[c, z] = sz[c, z]
        total = rz[c, 0].astype(F32)
        for i in range(1, Z):
            total = total + rz[c, i].astype(F32)
        out[c, core, x, z] = total.astype(BF)
        others(Z, z, lambda i: az_copy(c, i, z).start())

    def stage_ax(c):
        others(Z, z, lambda i: az_copy(c, i, i).wait_recv())
        others(X, x, lambda i: ax_copy(c, i, x).start())

    def stage_ac(c):
        others(X, x, lambda i: ax_copy(c, i, i).wait_recv())
        ac_copy(c, core).start()

    def stage_last(c):
        ac_copy(c, 1 - core).wait_recv()
        out_store(c).start()

    def stage_end(c):
        core_copy(c).wait_send()
        others(X, x, lambda i: x_copy(c, i, x).wait_send())
        others(Z, z, lambda i: z_copy(c, i, z).wait_send())
        others(Z, z, lambda i: az_copy(c, i, z).wait_send())
        others(X, x, lambda i: ax_copy(c, i, x).wait_send())
        ac_copy(c, core).wait_send()

    weight(0, gv)
    stage_core(0)

    inside(gqa, gs, v, k, False, 0)
    stage_x(0)
    send_g.wait()
    keep_g = jnp.where(me == N - 1, 0.0, 1.0)
    gk32[length : length + 8, :] = edge_gr[0:8, :].astype(F32) * keep_g

    sums = [jnp.zeros((8, D), F32)] * TAPS
    for i in range(tiles):
        start = i * TILE
        rows = gk32[start : start + TILE + 8, :]
        keys = kp32[start : start + TILE + 8, :]
        own = rows[0:TILE]
        total = taps[0:1] * own
        for j in range(1, TAPS):
            total = total + taps[j : j + 1] * rows[j : j + TILE]
        gp[start : start + TILE, :] = total.astype(BF)
        sums = [
            sums[j] + jnp.sum((own * keys[8 - j : 8 - j + TILE]).reshape(TILE // 8, 8, D), 0)
            for j in range(TAPS)
        ]
    for j in range(TAPS):
        csend[0, j : j + 1, :] = jnp.sum(sums[j], 0, keepdims=True)

    conv_core = remote(csend.at[0], crc, cv_c.at[0], cv_c.at[1], {"outer": x * 2 + 1 - core})

    def conv_x(i, source):
        return remote(csend.at[1], crx.at[source], cv_x.at[0, i], cv_x.at[1, source],
                      {"outer": i * 2 + core})

    def conv_z(i, source):
        return remote(csend.at[2], crz.at[source], cv_z.at[0, i], cv_z.at[1, source], {"seq": i})

    weight(2, gp)
    stage_core(2)
    conv_core.start()
    inside(gqa, gs, v, k, False, 1)
    stage_x(2)
    conv_core.wait_recv()
    csend[1] = csend[0] + crc[...]
    others(X, x, lambda i: conv_x(i, x).start())

    take(st, 0, s2_recv)
    for p in range(PAIRS):
        prev = from_parts(0, p)
        for b in range(blocks):
            sp[b, p] = jnp.concatenate([prev * low, prev * high], 0).astype(BF)
            prev = prev + kvb[b, p]
    for b, p, rows, lanes in spots:
        gq[rows, lanes] = (gqa[rows, lanes] + mm(gs[rows, lanes], sp[b, p], NT)).astype(BF)
    weight(1, gq)
    stage_core(1)
    stage_z(0)

    def gin_part(part):
        rows = slice(part * length // 2, (part + 1) * length // 2)
        total = mm(gq[rows, :], wq[...], NT)
        total = total + mm(gv[rows, :], wv[...], NT)
        total = total + mm(gp[rows, :], wk[...], NT)
        gin[rows, :] = total.astype(BF)

    def gin_store(part):
        rows = slice(part * length // 2, (part + 1) * length // 2)
        return pltpu.make_async_copy(gin.at[rows], gin_hbm.at[rows], out_sem.at[part])

    def out_store(c):
        return pltpu.make_async_copy(out.at[c], out_hbm.at[c], out_sem.at[2 + c])

    gin_part(0)
    gin_store(0).start()
    stage_x(1)
    gin_part(1)
    gin_store(1).start()
    stage_z(2)
    stage_az(0)
    stage_z(1)
    stage_az(2)
    stage_ax(0)
    stage_az(1)
    stage_ac(0)
    stage_ax(2)
    others(X, x, lambda i: conv_x(i, i).wait_recv())
    crx[x] = csend[1]
    total = crx[0]
    for i in range(1, X):
        total = total + crx[i]
    csend[2] = total
    others(Z, z, lambda i: conv_z(i, z).start())
    stage_ax(1)
    stage_ac(2)
    others(Z, z, lambda i: conv_z(i, i).wait_recv())
    crz[z] = csend[2]
    total = crz[0]
    for i in range(1, Z):
        total = total + crz[i]
    conv_out[...] = total
    conv_store = pltpu.make_async_copy(conv_out, conv_hbm, out_sem.at[5])
    conv_store.start()
    stage_last(0)
    stage_ac(1)
    stage_last(2)
    stage_last(1)
    for kind in range(2):
        take(sb, kind, s1_send)
        take(so, kind, s2_send)
    conv_core.wait_send()
    others(X, x, lambda i: conv_x(i, x).wait_send())
    others(Z, z, lambda i: conv_z(i, z).wait_send())
    stage_end(0)
    stage_end(1)
    stage_end(2)
    gin_store(0).wait()
    gin_store(1).wait()
    conv_store.wait()
    for c in range(3):
        out_store(c).wait()


def on_device(seq_count, outer_count, inputs, grad_out, w_query, w_key, w_value, conv_taps):
    length = inputs.shape[0]
    Z, X = seq_count, outer_count // 2
    N = seq_count * outer_count
    r = D // N
    blocks = length // BLOCK
    vm = pltpu.VMEM
    dma = pltpu.SemaphoreType.DMA
    full = vm((length, D), BF)
    edge = vm((EDGE, D), BF)
    weight = vm((D, D), BF)
    state = vm((blocks, PAIRS, HEAD_DIM, PAIR), F32)
    shared = vm((2, N, PAIRS * HEAD_DIM // N, PAIR), BF)
    square = vm((blocks, PAIRS, PAIR, PAIR), BF)
    scratch = [
        full, full, weight, weight, weight, vm((TAPS, D), BF),
        full, vm((3, 2, X, Z, r, D), BF), vm((TAPS, D), F32),
        vm((length + 8, D), F32), full, full, full, full, full,
        vm((length, D), F32), vm((length, D), F32), vm((length, D), F32), full,
        vm((length + 8, D), F32), full, full,
        edge, edge, edge,
        state, state, shared, shared, shared, shared, square, square,
        vm((3, 2, X, Z, r, D), BF), vm((3, X, Z, r, D), BF), vm((3, X, Z, r, D), BF),
        vm((3, X, Z, r, D), BF), vm((3, Z, r, D), BF), vm((3, Z, r, D), BF),
        vm((3, TAPS, D), F32), vm((TAPS, D), F32), vm((X, TAPS, D), F32), vm((Z, TAPS, D), F32),
        dma((4,)), dma((2,)), dma((2,)), dma((2,)), dma((2,)),
        dma((2,)), dma((2, X)), dma((2, Z)),
        dma((3, 2)), dma((3, X)), dma((3, X)), dma((3, Z)), dma((3, Z)),
        dma((3, Z)), dma((3, Z)), dma((3, X)), dma((3, X)), dma((3, 2)),
        dma((6,)), dma((6,)),
    ]
    spec = pl.BlockSpec(memory_space=pl.ANY)
    grad_inputs, weights, grad_conv = pl.pallas_call(
        functools.partial(kernel, seq_count, outer_count),
        out_shape=(
            jax.ShapeDtypeStruct((length, D), BF),
            jax.ShapeDtypeStruct((3, 2, X, Z, r, D), BF),
            jax.ShapeDtypeStruct((TAPS, D), F32),
        ),
        in_specs=[spec] * 6,
        out_specs=(spec, spec, spec),
        scratch_shapes=scratch,
        compiler_params=pltpu.CompilerParams(
            collective_id=0, has_side_effects=True, vmem_limit_bytes=56 * 1024 * 1024
        ),
    )(inputs, grad_out, w_query, w_key, w_value, conv_taps)
    weights = weights.reshape(3, D, D).astype(F32)
    return (grad_inputs, weights[1], weights[2], weights[0], grad_conv)


def solution(mesh):
    rows = P(("grp", "outer", "seq"), None)
    body = functools.partial(on_device, mesh.shape["seq"], mesh.shape["outer"])
    return jax.shard_map(
        body,
        mesh=mesh,
        in_specs=(rows, rows, P(), P(), P(), P()),
        out_specs=(rows, P("grp", None), P("grp", None), P("grp", None), P("grp", None)),
        check_vma=False,
    )
```

```python
import functools
import math

import jax
import jax.numpy as jnp
from jax import lax
from jax.experimental import pallas as pl
from jax.experimental.pallas import tpu as pltpu
from jax.sharding import PartitionSpec as P

D = 512
HEADS = 8
HEAD_DIM = 64
TAPS = 4
BLOCK = 512
STRIP = 128
TILE = 256
PAIR = 2 * HEAD_DIM
PAIRS = D // PAIR
EDGE = 16
MESH = pl.DeviceIdType.MESH
BF = jnp.bfloat16
F32 = jnp.float32

NN = (((1,), (0,)), ((), ()))
NT = (((1,), (1,)), ((), ()))
TN = (((0,), (0,)), ((), ()))


def mm(a, b, dims):
    return lax.dot_general(a, b, dims, preferred_element_type=F32)


def kernel(
    seq_count, outer_count,
    inp_hbm, go_hbm, wq_hbm, wk_hbm, wv_hbm, taps_hbm,
    gin_hbm, out_hbm, conv_hbm,
    inp, go, wq, wk, wv, taps_ref, gin, out, conv_out,
    kp32, q, qs, k, v, gs, gva, gqa, gka, gq, gk32, gv, gp,
    edge_k, edge_g, edge_gr,
    kvb, qdb, sb, rb, so, st, sp, sn,
    wb, rc, sx, rx, sz, rz, csend, crc, crx, crz,
    edge_sem, s1_send, s1_recv, s2_send, s2_recv, cv_c, cv_x, cv_z,
    c_sem, x_send, x_recv, z_send, z_recv, az_send, az_recv, ax_send, ax_recv, ac_sem,
    in_sem, out_sem,
):
    Z = seq_count
    X = outer_count // 2
    N = seq_count * outer_count
    length = inp.shape[0]
    blocks = length // BLOCK
    tiles = length // TILE
    r = D // N
    share = PAIRS * HEAD_DIM // N
    z = lax.axis_index("seq")
    o = lax.axis_index("outer")
    x, core = o // 2, o % 2
    me = o * Z + z

    def at(place):
        return {"seq": place % Z, "outer": place // Z}

    def others(count, mine, body):
        def one(i, carry):
            @pl.when(i != mine)
            def _():
                body(i)
            return carry
        lax.fori_loop(0, count, one, 0)

    def remote(src, dst, send, recv, device):
        return pltpu.make_async_remote_copy(
            src_ref=src, dst_ref=dst, send_sem=send, recv_sem=recv,
            device_id=device, device_id_type=MESH,
        )

    def peers(body):
        def one(i, carry):
            body(lax.rem(me + i, N))
            return carry
        lax.fori_loop(1, N, one, 0, unroll=N <= 16)

    operands = (
        (inp_hbm, inp), (wq_hbm, wq), (go_hbm, go), (wk_hbm, wk), (wv_hbm, wv), (taps_hbm, taps_ref)
    )
    loads = [pltpu.make_async_copy(a, b, in_sem.at[i]) for i, (a, b) in enumerate(operands)]
    for load in loads:
        load.start()
    inp_load, wq_load, go_load, wk_load, wv_load, taps_load = loads

    barrier = pltpu.get_barrier_semaphore()
    after, ahead = (me + 1) % N, (me + N - 1) % N

    def greet(place):
        pl.semaphore_signal(barrier, inc=1, device_id=at(place), device_id_type=MESH)

    peers(greet)

    lane = lax.broadcasted_iota(jnp.int32, (1, PAIR), 1)
    low = jnp.where(lane < HEAD_DIM, 1.0, 0.0)
    high = 1.0 - low
    masks = (low.astype(BF), high.astype(BF))

    inp_load.wait()
    wq_load.wait()
    q[...] = mm(inp[...], wq[...], NN).astype(BF)
    go_load.wait()
    for i in range(tiles):
        rows = slice(i * TILE, (i + 1) * TILE)
        place = lax.broadcasted_iota(jnp.int32, (TILE, 128), 0) + (me * length + i * TILE)
        scale = 1.0 / (jnp.sqrt(place.astype(F32) + 1.0) * math.sqrt(HEAD_DIM))
        scale = jnp.concatenate([scale] * (D // 128), 1)
        qs[rows, :] = (q[rows, :].astype(F32) * scale).astype(BF)
        gs[rows, :] = (go[rows, :].astype(F32) * scale).astype(BF)

    def shrink(full):
        return full[:HEAD_DIM] * low + full[HEAD_DIM:] * high

    def block_states(kind, first, second, kept):
        for p in range(PAIRS):
            cols = slice(p * PAIR, (p + 1) * PAIR)
            total = None
            for b in range(blocks):
                rows = slice(b * BLOCK, (b + 1) * BLOCK)
                one = shrink(mm(first[rows, cols], second[rows, cols], TN))
                kept[b, p] = one
                total = one if total is None else total + one
            per = HEAD_DIM // share
            sb[kind, p * per : (p + 1) * per] = total.reshape(per, share, PAIR).astype(BF)

    def to_owner(kind, i):
        return remote(sb.at[kind, i], rb.at[kind, me], s1_send.at[kind], s1_recv.at[kind], at(i))

    def to_member(kind, i):
        return remote(so.at[kind, i], st.at[kind, me], s2_send.at[kind], s2_recv.at[kind], at(i))

    def take(buffer, kind, sem):
        whole = buffer.at[kind, pl.ds(0, N - 1)]
        pltpu.make_async_copy(whole, whole, sem.at[kind]).wait()

    def send_states(kind):
        rb[kind, me] = sb[kind, me]
        peers(lambda i: to_owner(kind, i).start())

    def return_states(kind):
        take(rb, kind, s1_recv)
        total = jnp.zeros((share, PAIR), F32)
        for i in reversed(range(N)) if kind else range(N):
            so[kind, i] = total.astype(BF)
            total = total + rb[kind, i].astype(F32)
        st[kind, me] = so[kind, me]
        peers(lambda i: to_member(kind, i).start())

    block_states(1, qs, go, qdb)
    pl.semaphore_wait(barrier, N - 1)
    send_k = remote(inp_hbm.at[length - EDGE : length], edge_k, edge_sem.at[0], edge_sem.at[1], at(after))
    send_k.start()
    send_states(1)
    wk_load.wait()
    kp32[8 : 8 + length, :] = mm(inp[...], wk[...], NN).astype(BF).astype(F32)
    wv_load.wait()
    v[...] = mm(inp[...], wv[...], NN).astype(BF)
    row = lax.broadcasted_iota(jnp.int32, (STRIP, 2 * STRIP), 0)
    col = lax.broadcasted_iota(jnp.int32, (STRIP, 2 * STRIP), 1) % STRIP

    def attend(first, second, third, keys_first, b, p):
        lanes = slice(p * PAIR, (p + 1) * PAIR)
        base = b * BLOCK
        causal = row <= col if keys_first else row >= col
        whole = first[base : base + BLOCK, lanes]
        strips = BLOCK // STRIP
        total = None
        for j in reversed(range(strips)) if keys_first else range(strips):
            cut = slice(base + j * STRIP, base + (j + 1) * STRIP)
            b_part, c_part = second[cut, lanes], third[cut, lanes]
            right = jnp.concatenate([b_part * mask for mask in masks], 0)
            weights = jnp.concatenate([c_part * mask for mask in masks], 0)
            if keys_first:
                last = (j + 1) * STRIP
                score = mm(whole[:last], right, NT)
                part = jnp.where(causal, score[j * STRIP :], 0.0).astype(BF)
                if j > 0:
                    part = jnp.concatenate([score[: j * STRIP].astype(BF), part], 0)
                res = mm(part, weights, NN)
                if total is None:
                    total = res
                else:
                    total = jnp.concatenate([total[:last] + res, total[last:]], 0)
            else:
                begin = j * STRIP
                score = mm(whole[begin:], right, NT)
                part = jnp.where(causal, score[:STRIP], 0.0).astype(BF)
                if j < strips - 1:
                    part = jnp.concatenate([part, score[STRIP:].astype(BF)], 0)
                res = mm(part, weights, NN)
                if total is None:
                    total = res
                else:
                    total = jnp.concatenate([total[:begin], total[begin:] + res], 0)
        return total

    spots = [
        (b, p, slice(b * BLOCK, (b + 1) * BLOCK), slice(p * PAIR, (p + 1) * PAIR))
        for b in range(blocks) for p in range(PAIRS)
    ]

    def inside(total, first, second, third, keys_first, part):
        for b, p, rows, lanes in spots[part * len(spots) // 2 : (part + 1) * len(spots) // 2]:
            total[rows, lanes] = attend(first, second, third, keys_first, b, p)

    per = HEAD_DIM // share

    def from_parts(kind, p):
        return st[kind, p * per : (p + 1) * per].astype(F32).reshape(HEAD_DIM, PAIR)

    inside(gka, v, gs, q, True, 0)
    inside(gka, v, gs, q, True, 1)
    taps_load.wait()
    taps = taps_ref[...].astype(F32)
    send_k.wait()
    keep = jnp.where(me == 0, 0.0, 1.0)
    edge = mm(edge_k[...], wk[...], NN).astype(BF).astype(F32)
    kp32[0:8, :] = edge[EDGE - 8 : EDGE] * keep
    for i in range(tiles):
        start = i * TILE
        rows = kp32[start : start + TILE + 8, :]
        total = taps[0:1] * rows[8 : 8 + TILE]
        for j in range(1, TAPS):
            total = total + taps[j : j + 1] * rows[8 - j : 8 - j + TILE]
        k[start : start + TILE, :] = total.astype(BF)

    block_states(0, k, v, kvb)
    send_states(0)
    return_states(1)
    inside(gva, k, qs, go, True, 0)
    inside(gva, k, qs, go, True, 1)
    inside(gqa, gs, v, k, False, 0)
    return_states(0)

    take(st, 1, s2_recv)
    for p in range(PAIRS):
        later = from_parts(1, p)
        for b in reversed(range(blocks)):
            sn[b, p] = jnp.concatenate([later * low, later * high], 0).astype(BF)
            later = later + qdb[b, p]

    for b, p, rows, lanes in spots:
        gk32[rows, lanes] = (gka[rows, lanes] + mm(v[rows, lanes], sn[b, p], NT)).astype(BF).astype(F32)
        if b == 0 and p == PAIRS - 1:
            edge_g[...] = gk32[0:EDGE, :].astype(BF)
            send_g = remote(edge_g, edge_gr, edge_sem.at[2], edge_sem.at[3], at(ahead))
            send_g.start()
    for b, p, rows, lanes in spots:
        gv[rows, lanes] = (gva[rows, lanes] + mm(k[rows, lanes], sn[b, p], NN)).astype(BF)

    def weight(c, grads):
        res = mm(inp[...], grads[...], TN).astype(BF)
        for i in range(2 * X * Z):
            wb[c, i // (X * Z), i // Z % X, i % Z] = res[r * i : r * i + r]

    def core_copy(c):
        return remote(wb.at[c, 1 - core], rc.at[c], c_sem.at[c, 0], c_sem.at[c, 1],
                      {"outer": x * 2 + 1 - core})

    def x_copy(c, i, source):
        return remote(sx.at[c, i], rx.at[c, source], x_send.at[c, i], x_recv.at[c, source],
                      {"outer": i * 2 + core})

    def z_copy(c, i, source):
        return remote(sz.at[c, i], rz.at[c, source], z_send.at[c, i], z_recv.at[c, source],
                      {"seq": i})

    def az_copy(c, i, source):
        slot = out.at[c, core, x, source]
        return remote(slot, slot, az_send.at[c, i], az_recv.at[c, source], {"seq": i})

    def ax_copy(c, i, source):
        slot = out.at[c, core, source]
        return remote(slot, slot, ax_send.at[c, i], ax_recv.at[c, source],
                      {"outer": i * 2 + core})

    def ac_copy(c, source):
        slot = out.at[c, source]
        return remote(slot, slot, ac_sem.at[c, 0], ac_sem.at[c, 1],
                      {"outer": x * 2 + 1 - core})

    def stage_core(c):
        core_copy(c).start()

    def stage_x(c):
        core_copy(c).wait_recv()
        for i in range(X):
            sx[c, i] = (wb[c, core, i].astype(F32) + rc[c, i].astype(F32)).astype(BF)
        others(X, x, lambda i: x_copy(c, i, x).start())

    def stage_z(c):
        others(X, x, lambda i: x_copy(c, i, i).wait_recv())
        rx[c, x] = sx[c, x]
        total = rx[c, 0].astype(F32)
        for i in range(1, X):
            total = total + rx[c, i].astype(F32)
        sz[c] = total.astype(BF)
        others(Z, z, lambda i: z_copy(c, i, z).start())

    def stage_az(c):
        others(Z, z, lambda i: z_copy(c, i, i).wait_recv())
        rz[c, z] = sz[c, z]
        total = rz[c, 0].astype(F32)
        for i in range(1, Z):
            total = total + rz[c, i].astype(F32)
        out[c, core, x, z] = total.astype(BF)
        others(Z, z, lambda i: az_copy(c, i, z).start())

    def stage_ax(c):
        others(Z, z, lambda i: az_copy(c, i, i).wait_recv())
        others(X, x, lambda i: ax_copy(c, i, x).start())

    def stage_ac(c):
        others(X, x, lambda i: ax_copy(c, i, i).wait_recv())
        ac_copy(c, core).start()

    def stage_last(c):
        ac_copy(c, 1 - core).wait_recv()
        out_store(c).start()

    def stage_end(c):
        core_copy(c).wait_send()
        others(X, x, lambda i: x_copy(c, i, x).wait_send())
        others(Z, z, lambda i: z_copy(c, i, z).wait_send())
        others(Z, z, lambda i: az_copy(c, i, z).wait_send())
        others(X, x, lambda i: ax_copy(c, i, x).wait_send())
        ac_copy(c, core).wait_send()

    weight(0, gv)
    stage_core(0)

    inside(gqa, gs, v, k, False, 1)
    stage_x(0)
    send_g.wait()
    keep_g = jnp.where(me == N - 1, 0.0, 1.0)
    gk32[length : length + 8, :] = edge_gr[0:8, :].astype(F32) * keep_g

    for i in range(tiles):
        start = i * TILE
        rows = gk32[start : start + TILE + 8, :]
        total = taps[0:1] * rows[0:TILE]
        for j in range(1, TAPS):
            total = total + taps[j : j + 1] * rows[j : j + TILE]
        gp[start : start + TILE, :] = total.astype(BF)

    conv_core = remote(csend.at[0], crc, cv_c.at[0], cv_c.at[1], {"outer": x * 2 + 1 - core})

    def conv_x(i, source):
        return remote(csend.at[1], crx.at[source], cv_x.at[0, i], cv_x.at[1, source],
                      {"outer": i * 2 + core})

    def conv_z(i, source):
        return remote(csend.at[2], crz.at[source], cv_z.at[0, i], cv_z.at[1, source], {"seq": i})

    weight(2, gp)
    stage_core(2)
    take(st, 0, s2_recv)
    for p in range(PAIRS):
        prev = from_parts(0, p)
        for b in range(blocks):
            sp[b, p] = jnp.concatenate([prev * low, prev * high], 0).astype(BF)
            prev = prev + kvb[b, p]
    for b, p, rows, lanes in spots:
        gq[rows, lanes] = (gqa[rows, lanes] + mm(gs[rows, lanes], sp[b, p], NT)).astype(BF)
    weight(1, gq)
    stage_core(1)
    stage_x(2)
    sums = [jnp.zeros((8, D), F32)] * TAPS
    for i in range(tiles):
        start = i * TILE
        own = gk32[start : start + TILE, :]
        keys = kp32[start : start + TILE + 8, :]
        sums = [
            sums[j] + jnp.sum((own * keys[8 - j : 8 - j + TILE]).reshape(TILE // 8, 8, D), 0)
            for j in range(TAPS)
        ]
    for j in range(TAPS):
        csend[0, j : j + 1, :] = jnp.sum(sums[j], 0, keepdims=True)
    conv_core.start()
    stage_x(1)
    stage_z(0)

    def gin_part(part):
        rows = slice(part * length // 2, (part + 1) * length // 2)
        total = mm(gq[rows, :], wq[...], NT)
        total = total + mm(gv[rows, :], wv[...], NT)
        total = total + mm(gp[rows, :], wk[...], NT)
        gin[rows, :] = total.astype(BF)

    def gin_store(part):
        rows = slice(part * length // 2, (part + 1) * length // 2)
        return pltpu.make_async_copy(gin.at[rows], gin_hbm.at[rows], out_sem.at[part])

    def out_store(c):
        return pltpu.make_async_copy(out.at[c], out_hbm.at[c], out_sem.at[2 + c])

    gin_part(0)
    gin_store(0).start()
    conv_core.wait_recv()
    csend[1] = csend[0] + crc[...]
    others(X, x, lambda i: conv_x(i, x).start())
    gin_part(1)
    gin_store(1).start()
    stage_z(2)
    stage_az(0)
    stage_z(1)
    stage_az(2)
    stage_ax(0)
    stage_az(1)
    stage_ac(0)
    stage_ax(2)
    others(X, x, lambda i: conv_x(i, i).wait_recv())
    crx[x] = csend[1]
    total = crx[0]
    for i in range(1, X):
        total = total + crx[i]
    csend[2] = total
    others(Z, z, lambda i: conv_z(i, z).start())
    stage_ax(1)
    stage_ac(2)
    others(Z, z, lambda i: conv_z(i, i).wait_recv())
    crz[z] = csend[2]
    total = crz[0]
    for i in range(1, Z):
        total = total + crz[i]
    conv_out[...] = total
    conv_store = pltpu.make_async_copy(conv_out, conv_hbm, out_sem.at[5])
    conv_store.start()
    stage_last(0)
    stage_ac(1)
    stage_last(2)
    stage_last(1)
    for kind in range(2):
        take(sb, kind, s1_send)
        take(so, kind, s2_send)
    conv_core.wait_send()
    others(X, x, lambda i: conv_x(i, x).wait_send())
    others(Z, z, lambda i: conv_z(i, z).wait_send())
    stage_end(0)
    stage_end(1)
    stage_end(2)
    gin_store(0).wait()
    gin_store(1).wait()
    conv_store.wait()
    for c in range(3):
        out_store(c).wait()


def on_device(seq_count, outer_count, inputs, grad_out, w_query, w_key, w_value, conv_taps):
    length = inputs.shape[0]
    Z, X = seq_count, outer_count // 2
    N = seq_count * outer_count
    r = D // N
    blocks = length // BLOCK
    vm = pltpu.VMEM
    dma = pltpu.SemaphoreType.DMA
    full = vm((length, D), BF)
    edge = vm((EDGE, D), BF)
    weight = vm((D, D), BF)
    state = vm((blocks, PAIRS, HEAD_DIM, PAIR), F32)
    shared = vm((2, N, PAIRS * HEAD_DIM // N, PAIR), BF)
    square = vm((blocks, PAIRS, PAIR, PAIR), BF)
    scratch = [
        full, full, weight, weight, weight, vm((TAPS, D), BF),
        full, vm((3, 2, X, Z, r, D), BF), vm((TAPS, D), F32),
        vm((length + 8, D), F32), full, full, full, full, full,
        vm((length, D), F32), vm((length, D), F32), vm((length, D), F32), full,
        vm((length + 8, D), F32), full, full,
        edge, edge, edge,
        state, state, shared, shared, shared, shared, square, square,
        vm((3, 2, X, Z, r, D), BF), vm((3, X, Z, r, D), BF), vm((3, X, Z, r, D), BF),
        vm((3, X, Z, r, D), BF), vm((3, Z, r, D), BF), vm((3, Z, r, D), BF),
        vm((3, TAPS, D), F32), vm((TAPS, D), F32), vm((X, TAPS, D), F32), vm((Z, TAPS, D), F32),
        dma((4,)), dma((2,)), dma((2,)), dma((2,)), dma((2,)),
        dma((2,)), dma((2, X)), dma((2, Z)),
        dma((3, 2)), dma((3, X)), dma((3, X)), dma((3, Z)), dma((3, Z)),
        dma((3, Z)), dma((3, Z)), dma((3, X)), dma((3, X)), dma((3, 2)),
        dma((6,)), dma((6,)),
    ]
    spec = pl.BlockSpec(memory_space=pl.ANY)
    grad_inputs, weights, grad_conv = pl.pallas_call(
        functools.partial(kernel, seq_count, outer_count),
        out_shape=(
            jax.ShapeDtypeStruct((length, D), BF),
            jax.ShapeDtypeStruct((3, 2, X, Z, r, D), BF),
            jax.ShapeDtypeStruct((TAPS, D), F32),
        ),
        in_specs=[spec] * 6,
        out_specs=(spec, spec, spec),
        scratch_shapes=scratch,
        compiler_params=pltpu.CompilerParams(
            collective_id=0, has_side_effects=True, vmem_limit_bytes=56 * 1024 * 1024
        ),
    )(inputs, grad_out, w_query, w_key, w_value, conv_taps)
    weights = weights.reshape(3, D, D).astype(F32)
    return (grad_inputs, weights[1], weights[2], weights[0], grad_conv)


def solution(mesh):
    rows = P(("grp", "outer", "seq"), None)
    body = functools.partial(on_device, mesh.shape["seq"], mesh.shape["outer"])
    return jax.shard_map(
        body,
        mesh=mesh,
        in_specs=(rows, rows, P(), P(), P(), P()),
        out_specs=(rows, P("grp", None), P("grp", None), P("grp", None), P("grp", None)),
        check_vma=False,
    )
```

```python
import functools
import math

import jax
import jax.numpy as jnp
from jax import lax
from jax.experimental import pallas as pl
from jax.experimental.pallas import tpu as pltpu
from jax.sharding import PartitionSpec as P

D = 512
HEADS = 8
HEAD_DIM = 64
TAPS = 4
BLOCK = 512
STRIP = 128
TILE = 256
PAIR = 2 * HEAD_DIM
PAIRS = D // PAIR
EDGE = 16
MESH = pl.DeviceIdType.MESH
BF = jnp.bfloat16
F32 = jnp.float32

NN = (((1,), (0,)), ((), ()))
NT = (((1,), (1,)), ((), ()))
TN = (((0,), (0,)), ((), ()))


def mm(a, b, dims):
    return lax.dot_general(a, b, dims, preferred_element_type=F32)


def kernel(
    seq_count, outer_count,
    inp_hbm, go_hbm, wq_hbm, wk_hbm, wv_hbm, taps_hbm,
    gin_hbm, out_hbm, conv_hbm,
    inp, go, wq, wk, wv, taps_ref, gin, out, conv_out,
    kp32, q, qs, k, v, gs, gva, gqa, gka, gq, gk32, gv, gp,
    edge_k, edge_g, edge_gr,
    kvb, qdb, sb, rb, so, st, sp, sn,
    wb, rc, sx, rx, sz, rz, csend, crc, crx, crz,
    edge_sem, s1_send, s1_recv, s2_send, s2_recv, cv_c, cv_x, cv_z,
    c_sem, x_send, x_recv, z_send, z_recv, az_send, az_recv, ax_send, ax_recv, ac_sem,
    in_sem, out_sem,
):
    Z = seq_count
    X = outer_count // 2
    N = seq_count * outer_count
    length = inp.shape[0]
    blocks = length // BLOCK
    tiles = length // TILE
    r = D // N
    share = PAIRS * HEAD_DIM // N
    z = lax.axis_index("seq")
    o = lax.axis_index("outer")
    x, core = o // 2, o % 2
    me = o * Z + z

    def at(place):
        return {"seq": place % Z, "outer": place // Z}

    def others(count, mine, body):
        def one(i, carry):
            @pl.when(i != mine)
            def _():
                body(i)
            return carry
        lax.fori_loop(0, count, one, 0)

    def remote(src, dst, send, recv, device):
        return pltpu.make_async_remote_copy(
            src_ref=src, dst_ref=dst, send_sem=send, recv_sem=recv,
            device_id=device, device_id_type=MESH,
        )

    def peers(body):
        def one(i, carry):
            body(lax.rem(me + i, N))
            return carry
        lax.fori_loop(1, N, one, 0, unroll=N <= 16)

    operands = (
        (inp_hbm, inp), (wq_hbm, wq), (go_hbm, go), (wk_hbm, wk), (wv_hbm, wv), (taps_hbm, taps_ref)
    )
    loads = [pltpu.make_async_copy(a, b, in_sem.at[i]) for i, (a, b) in enumerate(operands)]
    for load in loads:
        load.start()
    inp_load, wq_load, go_load, wk_load, wv_load, taps_load = loads

    barrier = pltpu.get_barrier_semaphore()
    after, ahead = (me + 1) % N, (me + N - 1) % N

    def greet(place):
        pl.semaphore_signal(barrier, inc=1, device_id=at(place), device_id_type=MESH)

    peers(greet)

    lane = lax.broadcasted_iota(jnp.int32, (1, PAIR), 1)
    low = jnp.where(lane < HEAD_DIM, 1.0, 0.0)
    high = 1.0 - low
    masks = (low.astype(BF), high.astype(BF))

    inp_load.wait()
    wq_load.wait()
    q[...] = mm(inp[...], wq[...], NN).astype(BF)
    go_load.wait()
    for i in range(tiles):
        rows = slice(i * TILE, (i + 1) * TILE)
        place = lax.broadcasted_iota(jnp.int32, (TILE, 128), 0) + (me * length + i * TILE)
        scale = 1.0 / (jnp.sqrt(place.astype(F32) + 1.0) * math.sqrt(HEAD_DIM))
        scale = jnp.concatenate([scale] * (D // 128), 1)
        qs[rows, :] = (q[rows, :].astype(F32) * scale).astype(BF)
        gs[rows, :] = (go[rows, :].astype(F32) * scale).astype(BF)

    def shrink(full):
        return full[:HEAD_DIM] * low + full[HEAD_DIM:] * high

    def block_states(kind, first, second, kept):
        for p in range(PAIRS):
            cols = slice(p * PAIR, (p + 1) * PAIR)
            total = None
            for b in range(blocks):
                rows = slice(b * BLOCK, (b + 1) * BLOCK)
                one = shrink(mm(first[rows, cols], second[rows, cols], TN))
                kept[b, p] = one
                total = one if total is None else total + one
            per = HEAD_DIM // share
            sb[kind, p * per : (p + 1) * per] = total.reshape(per, share, PAIR).astype(BF)

    def to_owner(kind, i):
        return remote(sb.at[kind, i], rb.at[kind, me], s1_send.at[kind], s1_recv.at[kind], at(i))

    def to_member(kind, i):
        return remote(so.at[kind, i], st.at[kind, me], s2_send.at[kind], s2_recv.at[kind], at(i))

    def take(buffer, kind, sem):
        whole = buffer.at[kind, pl.ds(0, N - 1)]
        pltpu.make_async_copy(whole, whole, sem.at[kind]).wait()

    def send_states(kind):
        rb[kind, me] = sb[kind, me]
        peers(lambda i: to_owner(kind, i).start())

    def return_states(kind):
        take(rb, kind, s1_recv)
        total = jnp.zeros((share, PAIR), F32)
        for i in reversed(range(N)) if kind else range(N):
            so[kind, i] = total.astype(BF)
            total = total + rb[kind, i].astype(F32)
        st[kind, me] = so[kind, me]
        peers(lambda i: to_member(kind, i).start())

    block_states(1, qs, go, qdb)
    pl.semaphore_wait(barrier, N - 1)
    send_k = remote(inp_hbm.at[length - EDGE : length], edge_k, edge_sem.at[0], edge_sem.at[1], at(after))
    send_k.start()
    send_states(1)
    wk_load.wait()
    kp32[8 : 8 + length, :] = mm(inp[...], wk[...], NN).astype(BF).astype(F32)
    wv_load.wait()
    v[...] = mm(inp[...], wv[...], NN).astype(BF)
    row = lax.broadcasted_iota(jnp.int32, (STRIP, 2 * STRIP), 0)
    col = lax.broadcasted_iota(jnp.int32, (STRIP, 2 * STRIP), 1) % STRIP

    def attend(first, second, third, keys_first, b, p):
        lanes = slice(p * PAIR, (p + 1) * PAIR)
        base = b * BLOCK
        causal = row <= col if keys_first else row >= col
        whole = first[base : base + BLOCK, lanes]
        strips = BLOCK // STRIP
        total = None
        for j in reversed(range(strips)) if keys_first else range(strips):
            cut = slice(base + j * STRIP, base + (j + 1) * STRIP)
            b_part, c_part = second[cut, lanes], third[cut, lanes]
            right = jnp.concatenate([b_part * mask for mask in masks], 0)
            weights = jnp.concatenate([c_part * mask for mask in masks], 0)
            if keys_first:
                last = (j + 1) * STRIP
                score = mm(whole[:last], right, NT)
                part = jnp.where(causal, score[j * STRIP :], 0.0).astype(BF)
                if j > 0:
                    part = jnp.concatenate([score[: j * STRIP].astype(BF), part], 0)
                res = mm(part, weights, NN)
                if total is None:
                    total = res
                else:
                    total = jnp.concatenate([total[:last] + res, total[last:]], 0)
            else:
                begin = j * STRIP
                score = mm(whole[begin:], right, NT)
                part = jnp.where(causal, score[:STRIP], 0.0).astype(BF)
                if j < strips - 1:
                    part = jnp.concatenate([part, score[STRIP:].astype(BF)], 0)
                res = mm(part, weights, NN)
                if total is None:
                    total = res
                else:
                    total = jnp.concatenate([total[:begin], total[begin:] + res], 0)
        return total

    spots = [
        (b, p, slice(b * BLOCK, (b + 1) * BLOCK), slice(p * PAIR, (p + 1) * PAIR))
        for b in range(blocks) for p in range(PAIRS)
    ]

    def inside(total, first, second, third, keys_first, part):
        for b, p, rows, lanes in spots[part * len(spots) // 2 : (part + 1) * len(spots) // 2]:
            total[rows, lanes] = attend(first, second, third, keys_first, b, p)

    per = HEAD_DIM // share

    def from_parts(kind, p):
        return st[kind, p * per : (p + 1) * per].astype(F32).reshape(HEAD_DIM, PAIR)

    inside(gka, v, gs, q, True, 0)
    inside(gka, v, gs, q, True, 1)
    taps_load.wait()
    taps = taps_ref[...].astype(F32)
    send_k.wait()
    keep = jnp.where(me == 0, 0.0, 1.0)
    edge = mm(edge_k[...], wk[...], NN).astype(BF).astype(F32)
    kp32[0:8, :] = edge[EDGE - 8 : EDGE] * keep
    for i in range(tiles):
        start = i * TILE
        rows = kp32[start : start + TILE + 8, :]
        total = taps[0:1] * rows[8 : 8 + TILE]
        for j in range(1, TAPS):
            total = total + taps[j : j + 1] * rows[8 - j : 8 - j + TILE]
        k[start : start + TILE, :] = total.astype(BF)

    block_states(0, k, v, kvb)
    send_states(0)
    return_states(1)
    inside(gva, k, qs, go, True, 0)
    inside(gva, k, qs, go, True, 1)
    inside(gqa, gs, v, k, False, 0)
    return_states(0)

    take(st, 1, s2_recv)
    for p in range(PAIRS):
        later = from_parts(1, p)
        for b in reversed(range(blocks)):
            sn[b, p] = jnp.concatenate([later * low, later * high], 0).astype(BF)
            later = later + qdb[b, p]

    for b, p, rows, lanes in spots:
        gk32[rows, lanes] = (gka[rows, lanes] + mm(v[rows, lanes], sn[b, p], NT)).astype(BF).astype(F32)
        if b == 0 and p == PAIRS - 1:
            edge_g[...] = gk32[0:EDGE, :].astype(BF)
            send_g = remote(edge_g, edge_gr, edge_sem.at[2], edge_sem.at[3], at(ahead))
            send_g.start()
    for b, p, rows, lanes in spots:
        gv[rows, lanes] = (gva[rows, lanes] + mm(k[rows, lanes], sn[b, p], NN)).astype(BF)

    def weight(c, grads):
        res = mm(inp[...], grads[...], TN).astype(BF)
        for i in range(2 * X * Z):
            wb[c, i // (X * Z), i // Z % X, i % Z] = res[r * i : r * i + r]

    def core_copy(c):
        return remote(wb.at[c, 1 - core], rc.at[c], c_sem.at[c, 0], c_sem.at[c, 1],
                      {"outer": x * 2 + 1 - core})

    def x_copy(c, i, source):
        return remote(sx.at[c, i], rx.at[c, source], x_send.at[c, i], x_recv.at[c, source],
                      {"outer": i * 2 + core})

    def z_copy(c, i, source):
        return remote(sz.at[c, i], rz.at[c, source], z_send.at[c, i], z_recv.at[c, source],
                      {"seq": i})

    def az_copy(c, i, source):
        slot = out.at[c, core, x, source]
        return remote(slot, slot, az_send.at[c, i], az_recv.at[c, source], {"seq": i})

    def ax_copy(c, i, source):
        slot = out.at[c, core, source]
        return remote(slot, slot, ax_send.at[c, i], ax_recv.at[c, source],
                      {"outer": i * 2 + core})

    def ac_copy(c, source):
        slot = out.at[c, source]
        return remote(slot, slot, ac_sem.at[c, 0], ac_sem.at[c, 1],
                      {"outer": x * 2 + 1 - core})

    def stage_core(c):
        core_copy(c).start()

    def stage_x(c):
        core_copy(c).wait_recv()
        for i in range(X):
            sx[c, i] = (wb[c, core, i].astype(F32) + rc[c, i].astype(F32)).astype(BF)
        others(X, x, lambda i: x_copy(c, i, x).start())

    def stage_z(c):
        others(X, x, lambda i: x_copy(c, i, i).wait_recv())
        rx[c, x] = sx[c, x]
        total = rx[c, 0].astype(F32)
        for i in range(1, X):
            total = total + rx[c, i].astype(F32)
        sz[c] = total.astype(BF)
        others(Z, z, lambda i: z_copy(c, i, z).start())

    def stage_az(c):
        others(Z, z, lambda i: z_copy(c, i, i).wait_recv())
        rz[c, z] = sz[c, z]
        total = rz[c, 0].astype(F32)
        for i in range(1, Z):
            total = total + rz[c, i].astype(F32)
        out[c, core, x, z] = total.astype(BF)
        others(Z, z, lambda i: az_copy(c, i, z).start())

    def stage_ax(c):
        others(Z, z, lambda i: az_copy(c, i, i).wait_recv())
        others(X, x, lambda i: ax_copy(c, i, x).start())

    def stage_ac(c):
        others(X, x, lambda i: ax_copy(c, i, i).wait_recv())
        ac_copy(c, core).start()

    def stage_last(c):
        ac_copy(c, 1 - core).wait_recv()
        out_store(c).start()

    def stage_end(c):
        core_copy(c).wait_send()
        others(X, x, lambda i: x_copy(c, i, x).wait_send())
        others(Z, z, lambda i: z_copy(c, i, z).wait_send())
        others(Z, z, lambda i: az_copy(c, i, z).wait_send())
        others(X, x, lambda i: ax_copy(c, i, x).wait_send())
        ac_copy(c, core).wait_send()

    weight(0, gv)
    stage_core(0)

    inside(gqa, gs, v, k, False, 1)
    stage_x(0)
    send_g.wait()
    keep_g = jnp.where(me == N - 1, 0.0, 1.0)
    gk32[length : length + 8, :] = edge_gr[0:8, :].astype(F32) * keep_g

    for i in range(tiles):
        start = i * TILE
        rows = gk32[start : start + TILE + 8, :]
        total = taps[0:1] * rows[0:TILE]
        for j in range(1, TAPS):
            total = total + taps[j : j + 1] * rows[j : j + TILE]
        gp[start : start + TILE, :] = total.astype(BF)

    conv_core = remote(csend.at[0], crc, cv_c.at[0], cv_c.at[1], {"outer": x * 2 + 1 - core})

    def conv_x(i, source):
        return remote(csend.at[1], crx.at[source], cv_x.at[0, i], cv_x.at[1, source],
                      {"outer": i * 2 + core})

    def conv_z(i, source):
        return remote(csend.at[2], crz.at[source], cv_z.at[0, i], cv_z.at[1, source], {"seq": i})

    weight(2, gp)
    stage_core(2)
    take(st, 0, s2_recv)
    for p in range(PAIRS):
        prev = from_parts(0, p)
        for b in range(blocks):
            sp[b, p] = jnp.concatenate([prev * low, prev * high], 0).astype(BF)
            prev = prev + kvb[b, p]
    for b, p, rows, lanes in spots:
        gq[rows, lanes] = (gqa[rows, lanes] + mm(gs[rows, lanes], sp[b, p], NT)).astype(BF)
    weight(1, gq)
    stage_core(1)
    stage_x(2)
    stage_x(1)
    sums = [jnp.zeros((8, D), F32)] * TAPS
    for i in range(tiles):
        start = i * TILE
        own = gk32[start : start + TILE, :]
        keys = kp32[start : start + TILE + 8, :]
        sums = [
            sums[j] + jnp.sum((own * keys[8 - j : 8 - j + TILE]).reshape(TILE // 8, 8, D), 0)
            for j in range(TAPS)
        ]
    for j in range(TAPS):
        csend[0, j : j + 1, :] = jnp.sum(sums[j], 0, keepdims=True)
    conv_core.start()
    stage_z(0)

    def gin_part(part):
        rows = slice(part * length // 2, (part + 1) * length // 2)
        total = mm(gq[rows, :], wq[...], NT)
        total = total + mm(gv[rows, :], wv[...], NT)
        total = total + mm(gp[rows, :], wk[...], NT)
        gin[rows, :] = total.astype(BF)

    def gin_store(part):
        rows = slice(part * length // 2, (part + 1) * length // 2)
        return pltpu.make_async_copy(gin.at[rows], gin_hbm.at[rows], out_sem.at[part])

    def out_store(c):
        return pltpu.make_async_copy(out.at[c], out_hbm.at[c], out_sem.at[2 + c])

    gin_part(0)
    gin_store(0).start()
    conv_core.wait_recv()
    csend[1] = csend[0] + crc[...]
    others(X, x, lambda i: conv_x(i, x).start())
    gin_part(1)
    gin_store(1).start()
    stage_z(2)
    stage_az(0)
    stage_z(1)
    stage_az(2)
    stage_ax(0)
    stage_az(1)
    stage_ac(0)
    stage_ax(2)
    others(X, x, lambda i: conv_x(i, i).wait_recv())
    crx[x] = csend[1]
    total = crx[0]
    for i in range(1, X):
        total = total + crx[i]
    csend[2] = total
    others(Z, z, lambda i: conv_z(i, z).start())
    stage_ax(1)
    stage_ac(2)
    others(Z, z, lambda i: conv_z(i, i).wait_recv())
    crz[z] = csend[2]
    total = crz[0]
    for i in range(1, Z):
        total = total + crz[i]
    conv_out[...] = total
    conv_store = pltpu.make_async_copy(conv_out, conv_hbm, out_sem.at[5])
    conv_store.start()
    stage_last(0)
    stage_ac(1)
    stage_last(2)
    stage_last(1)
    for kind in range(2):
        take(sb, kind, s1_send)
        take(so, kind, s2_send)
    conv_core.wait_send()
    others(X, x, lambda i: conv_x(i, x).wait_send())
    others(Z, z, lambda i: conv_z(i, z).wait_send())
    stage_end(0)
    stage_end(1)
    stage_end(2)
    gin_store(0).wait()
    gin_store(1).wait()
    conv_store.wait()
    for c in range(3):
        out_store(c).wait()


def on_device(seq_count, outer_count, inputs, grad_out, w_query, w_key, w_value, conv_taps):
    length = inputs.shape[0]
    Z, X = seq_count, outer_count // 2
    N = seq_count * outer_count
    r = D // N
    blocks = length // BLOCK
    vm = pltpu.VMEM
    dma = pltpu.SemaphoreType.DMA
    full = vm((length, D), BF)
    edge = vm((EDGE, D), BF)
    weight = vm((D, D), BF)
    state = vm((blocks, PAIRS, HEAD_DIM, PAIR), F32)
    shared = vm((2, N, PAIRS * HEAD_DIM // N, PAIR), BF)
    square = vm((blocks, PAIRS, PAIR, PAIR), BF)
    scratch = [
        full, full, weight, weight, weight, vm((TAPS, D), BF),
        full, vm((3, 2, X, Z, r, D), BF), vm((TAPS, D), F32),
        vm((length + 8, D), F32), full, full, full, full, full,
        vm((length, D), F32), vm((length, D), F32), vm((length, D), F32), full,
        vm((length + 8, D), F32), full, full,
        edge, edge, edge,
        state, state, shared, shared, shared, shared, square, square,
        vm((3, 2, X, Z, r, D), BF), vm((3, X, Z, r, D), BF), vm((3, X, Z, r, D), BF),
        vm((3, X, Z, r, D), BF), vm((3, Z, r, D), BF), vm((3, Z, r, D), BF),
        vm((3, TAPS, D), F32), vm((TAPS, D), F32), vm((X, TAPS, D), F32), vm((Z, TAPS, D), F32),
        dma((4,)), dma((2,)), dma((2,)), dma((2,)), dma((2,)),
        dma((2,)), dma((2, X)), dma((2, Z)),
        dma((3, 2)), dma((3, X)), dma((3, X)), dma((3, Z)), dma((3, Z)),
        dma((3, Z)), dma((3, Z)), dma((3, X)), dma((3, X)), dma((3, 2)),
        dma((6,)), dma((6,)),
    ]
    spec = pl.BlockSpec(memory_space=pl.ANY)
    grad_inputs, weights, grad_conv = pl.pallas_call(
        functools.partial(kernel, seq_count, outer_count),
        out_shape=(
            jax.ShapeDtypeStruct((length, D), BF),
            jax.ShapeDtypeStruct((3, 2, X, Z, r, D), BF),
            jax.ShapeDtypeStruct((TAPS, D), F32),
        ),
        in_specs=[spec] * 6,
        out_specs=(spec, spec, spec),
        scratch_shapes=scratch,
        compiler_params=pltpu.CompilerParams(
            collective_id=0, has_side_effects=True, vmem_limit_bytes=56 * 1024 * 1024
        ),
    )(inputs, grad_out, w_query, w_key, w_value, conv_taps)
    weights = weights.reshape(3, D, D).astype(F32)
    return (grad_inputs, weights[1], weights[2], weights[0], grad_conv)


def solution(mesh):
    rows = P(("grp", "outer", "seq"), None)
    body = functools.partial(on_device, mesh.shape["seq"], mesh.shape["outer"])
    return jax.shard_map(
        body,
        mesh=mesh,
        in_specs=(rows, rows, P(), P(), P(), P()),
        out_specs=(rows, P("grp", None), P("grp", None), P("grp", None), P("grp", None)),
        check_vma=False,
    )
```
